32 devices in a mesh: dp: 8 (over z, x), ctx: 4 (over y, core).
Axes of the slice: x: 2, y: 2, z: 4, core: 2. Of those that a mesh axis runs over, the one named last changes fastest.
Arguments:
- block_input: bfloat16 [8, 512, 1088], P('dp', 'ctx'), may hold values from -6 to 6
- norm_one_gain: bfloat16 [1088], P('dp'), may hold values from 0.099609375 to 1.8984375
- norm_one_bias: bfloat16 [1088], P('dp'), may hold values from -1.796875 to 1.796875
- w_qkv: bfloat16 [1088, 3264], P('ctx', 'dp'), may hold values from -3 to 3
- bias_qv: bfloat16 [2176], P('dp'), may hold values from -1.1953125 to 1.1953125
- w_out: bfloat16 [1088, 1088], P('ctx', 'dp'), may hold values from -1.5 to 1.5
- bias_out: bfloat16 [1088], P('dp'), may hold values from -1.796875 to 1.796875
- norm_two_gain: bfloat16 [1088], P('dp'), may hold values from 0.099609375 to 1.8984375
- norm_two_bias: bfloat16 [1088], P('dp'), may hold values from -1.796875 to 1.796875
- w_up: bfloat16 [1088, 4352], P('ctx', 'dp'), may hold values from -0.1875 to 0.1875
- bias_up: bfloat16 [4352], P('dp'), may hold values from -1.796875 to 1.796875
- w_down: bfloat16 [4352, 1088], P('ctx', 'dp'), may hold values from -0.09375 to 0.09375
- bias_down: bfloat16 [1088], P('dp'), may hold values from -1.796875 to 1.796875
- cotangent: bfloat16 [8, 512, 1088], P('dp', 'ctx'), may hold values from -6 to 6
Outputs:
- block_output: bfloat16 [8, 512, 1088], P('dp', 'ctx')
- grad_input: float32 [8, 512, 1088], P('dp', 'ctx')
- grad_norm_one_gain: float32 [1088], P('dp')
- grad_norm_one_bias: float32 [1088], P('dp')
- grad_w_qkv: float32 [1088, 3264], P('ctx', 'dp')
- grad_bias_qv: float32 [2176], P('dp')
- grad_w_out: float32 [1088, 1088], P('ctx', 'dp')
- grad_bias_out: float32 [1088], P('dp')
- grad_norm_two_gain: float32 [1088], P('dp')
- grad_norm_two_bias: float32 [1088], P('dp')
- grad_w_up: float32 [1088, 4352], P('ctx', 'dp')
- grad_bias_up: float32 [4352], P('dp')
- grad_w_down: float32 [4352, 1088], P('ctx', 'dp')
- grad_bias_down: float32 [1088], P('dp')
The draws below stay inside these ranges and needn't reach their ends.
All inputs are finite; a program needn't handle non-finite values.
Results may differ from the reference program's by a relative error of at most 0.01.
Values may be sent and summed in bfloat16 or wider, within the bound.
A program may use at most 192 MiB of HBM per device.

```python
import jax
import jax.numpy as jnp
from jax import lax

D = 1088
HEADS = 17
HEAD_DIM = 64
FF = 4352
LENGTH = 512
SEQS = 8
TOKENS = 4096


def draw_w_qkv(key, part):
    standard = jax.random.truncated_normal(key, -4.0, 4.0, (D, 3 * D), jnp.float32) * float(D) ** (-0.5)
    return standard.astype(jnp.bfloat16)


def strengthened(values, rng, source, target, shards_of, factor):
    owner, partner = [(jnp.arange(values.shape[axis_at]) // (values.shape[axis_at] // shards_of)).reshape([-1 if axis == axis_at else 1 for axis in range(values.ndim)]) for axis_at in (source, target)]
    chosen = jax.random.permutation(rng, shards_of)[partner]
    strong = (owner == chosen) | (owner == (partner + shards_of // 2) % shards_of)
    return jnp.where(strong, factor * values, values)


def block_levels(key, extent, cuts, least, largest):
    def one(axis_at, parts):
        heights = jax.random.uniform(jax.random.fold_in(jax.random.fold_in(key, 6), axis_at), (parts,), jnp.float32, least / len(cuts), largest / len(cuts))
        return jnp.repeat(jnp.exp(heights), extent[axis_at] // parts).reshape((-1,) + (1,) * (len(extent) - axis_at - 1))

    loudness = one(*cuts[0])
    for cut in cuts[1:]:
        loudness = loudness * one(*cut)
    return loudness


def centred(stream_key, dims, deviation, bound, cuts=(), kind=jnp.bfloat16):
    level = block_levels(stream_key, dims, cuts, -0.22, 0.18) if cuts else 1.0
    values = jax.random.normal(stream_key, dims, jnp.float32) * deviation * level
    return jnp.minimum(jnp.maximum(values, -bound), bound).astype(kind)


def bell_draw_with(rng, shape, scale, most, split, heavy, held_as=jnp.bfloat16):
    values = scale * jax.random.normal(rng, shape, jnp.float32)
    if split:
        values = values * block_levels(rng, shape, split, -0.22, 0.18)
    return jnp.clip(strengthened(values, jax.random.fold_in(rng, 3), *heavy), -most, most).astype(held_as)


def setup_inputs(seed: int = 0) -> dict:
    arg_keys = jax.random.split(jax.random.key(seed), 15)
    return {
        "block_input": centred(arg_keys[0], (SEQS, LENGTH, D), 1.0, 6.0, ((0, 8), (1, 4))),
        "norm_one_gain": jnp.clip(1.0 + 0.18 * jax.random.normal(arg_keys[1], (D,), jnp.float32), 0.099609375, 1.8984375).astype(jnp.bfloat16),
        "norm_one_bias": centred(arg_keys[2], (D,), 0.3, 1.796875, ((0, 8),)),
        "w_qkv": draw_w_qkv(jax.random.fold_in(arg_keys[14], 71), 0),
        "bias_qv": centred(arg_keys[4], (2 * D,), 0.2, 1.1953125, ((0, 8),)),
        "w_out": centred(arg_keys[5], (D, D), (D // 64) ** -0.5, 1.5, ((0, 4), (1, 8))),
        "bias_out": centred(arg_keys[6], (D,), 0.3, 1.796875, ((0, 8),)),
        "norm_two_gain": jnp.clip(1.0 + 0.18 * jax.random.normal(arg_keys[7], (D,), jnp.float32), 0.099609375, 1.8984375).astype(jnp.bfloat16),
        "norm_two_bias": centred(arg_keys[8], (D,), 0.3, 1.796875, ((0, 8),)),
        "w_up": centred(arg_keys[9], (D, FF), D ** -0.5, 0.1875, ((0, 4), (1, 8))),
        "bias_up": centred(arg_keys[10], (FF,), 0.3, 1.796875, ((0, 8),)),
        "w_down": centred(arg_keys[11], (FF, D), FF ** -0.5, 0.09375, ((0, 4), (1, 8))),
        "bias_down": centred(arg_keys[12], (D,), 0.3, 1.796875, ((0, 8),)),
        "cotangent": bell_draw_with(arg_keys[13], (SEQS, LENGTH, D), 1.0, 6.0, ((0, 8), (1, 4)), (0, 2, 8, 2.0)),
    }


EPS = 1e-05
MASKED = -1e+30
INV_ROOT_TWO = 0.7071067811865476
INV_ROOT_TWO_PI = 0.3989422804014327

def norm_forward(rows_in, gain, shift):
    center = lax.optimization_barrier(jnp.mean(rows_in, axis=-1, keepdims=True))
    offset = rows_in - center
    spread = lax.optimization_barrier(jnp.mean(offset * offset, axis=-1, keepdims=True))
    inverse = lax.rsqrt(spread + EPS)
    scaled = offset * inverse
    normed = (scaled * gain.astype(jnp.float32) + shift.astype(jnp.float32)).astype(jnp.bfloat16)
    return (scaled, inverse, normed)

def norm_backward(upstream, scaled, inverse, gain):
    weighted = upstream * gain.astype(jnp.float32)
    first = lax.optimization_barrier(jnp.mean(weighted, axis=-1, keepdims=True))
    second = lax.optimization_barrier(jnp.mean(weighted * scaled, axis=-1, keepdims=True))
    return inverse * (weighted - first - scaled * second)

def gelu_value(pre):
    return 0.5 * pre * (1.0 + lax.erf(pre * INV_ROOT_TWO))

def gelu_slope(pre):
    return 0.5 * (1.0 + lax.erf(pre * INV_ROOT_TWO)) + pre * jnp.exp(-0.5 * pre * pre) * INV_ROOT_TWO_PI

def split_heads(block):
    return block.astype(jnp.float32).reshape(block.shape[0], HEADS, HEAD_DIM)

def reference(block_input, norm_one_gain, norm_one_bias, w_qkv, bias_qv, w_out, bias_out, norm_two_gain, norm_two_bias, w_up, bias_up, w_down, bias_down, cotangent):
    factor = float(HEAD_DIM) ** (-0.5)
    bias_float = bias_qv.astype(jnp.float32)
    qkv_bias = jnp.concatenate([bias_float[:D], jnp.zeros((D,), jnp.float32), bias_float[D:]])
    positions = jnp.arange(LENGTH, dtype=jnp.int32)
    allowed = positions[None, :] <= positions[:, None]

    def one_sequence(totals, pair):
        seq_in, seq_cot = pair
        inputs = seq_in.astype(jnp.float32)
        scaled_one, inverse_one, normed_one = norm_forward(inputs, norm_one_gain, norm_one_bias)
        projected = (jnp.dot(normed_one, w_qkv, preferred_element_type=jnp.float32) + qkv_bias).astype(jnp.bfloat16)
        query_heads = split_heads(projected[:, :D])
        key_heads = split_heads(projected[:, D:2 * D])
        value_heads = split_heads(projected[:, 2 * D:])
        scores = jnp.einsum('qhd,khd->hqk', query_heads, key_heads) * factor
        scores = jnp.where(allowed[None], scores, MASKED)
        peak = lax.optimization_barrier(jnp.max(scores, axis=-1, keepdims=True))
        log_total = peak + jnp.log(lax.optimization_barrier(jnp.sum(jnp.exp(scores - peak), axis=-1, keepdims=True)))
        probs = jnp.exp(scores - log_total)
        soft_weights = probs.astype(jnp.bfloat16)
        mixed = jnp.einsum('hqk,khd->qhd', soft_weights.astype(jnp.float32), value_heads).reshape(LENGTH, D).astype(jnp.bfloat16)
        residual = inputs + (jnp.dot(mixed, w_out, preferred_element_type=jnp.float32) + bias_out.astype(jnp.float32))
        scaled_two, inverse_two, normed_two = norm_forward(residual, norm_two_gain, norm_two_bias)
        hidden_pre = jnp.dot(normed_two, w_up, preferred_element_type=jnp.float32) + bias_up.astype(jnp.float32)
        hidden = gelu_value(hidden_pre).astype(jnp.bfloat16)
        result = residual + (jnp.dot(hidden, w_down, preferred_element_type=jnp.float32) + bias_down.astype(jnp.float32))
        output = result.astype(jnp.bfloat16)
        up_float = seq_cot.astype(jnp.float32)
        grad_down = jnp.dot(hidden.T, seq_cot, preferred_element_type=jnp.float32)
        grad_bias_down = lax.optimization_barrier(jnp.sum(up_float, axis=0))
        grad_hidden = jnp.dot(seq_cot, w_down.T, preferred_element_type=jnp.float32) * gelu_slope(hidden_pre)
        grad_hidden_low = grad_hidden.astype(jnp.bfloat16)
        grad_up = jnp.dot(normed_two.T, grad_hidden_low, preferred_element_type=jnp.float32)
        grad_bias_up = lax.optimization_barrier(jnp.sum(grad_hidden, axis=0))
        grad_normed_two = jnp.dot(grad_hidden_low, w_up.T, preferred_element_type=jnp.float32)
        grad_gain_two = lax.optimization_barrier(jnp.sum(grad_normed_two * scaled_two, axis=0))
        grad_shift_two = lax.optimization_barrier(jnp.sum(grad_normed_two, axis=0))
        grad_residual = up_float + norm_backward(grad_normed_two, scaled_two, inverse_two, norm_two_gain)
        grad_residual_low = grad_residual.astype(jnp.bfloat16)
        grad_out = jnp.dot(mixed.T, grad_residual_low, preferred_element_type=jnp.float32)
        grad_bias_out = lax.optimization_barrier(jnp.sum(grad_residual, axis=0))
        grad_mixed = jnp.dot(grad_residual_low, w_out.T, preferred_element_type=jnp.float32).astype(jnp.bfloat16)
        mixed_heads = split_heads(grad_mixed)
        grad_probs = jnp.einsum('qhd,khd->hqk', mixed_heads, value_heads)
        delta = jnp.einsum('qhd,qhd->hq', mixed_heads, split_heads(mixed))[..., None]
        grad_scores = (probs * (grad_probs - delta) * factor).astype(jnp.bfloat16).astype(jnp.float32)
        grad_queries = jnp.einsum('hqk,khd->qhd', grad_scores, key_heads).reshape(LENGTH, D)
        grad_keys = jnp.einsum('hqk,qhd->khd', grad_scores, query_heads).reshape(LENGTH, D)
        grad_values = jnp.einsum('hqk,qhd->khd', soft_weights.astype(jnp.float32), mixed_heads).reshape(LENGTH, D)
        grad_bias_qv = jnp.concatenate([lax.optimization_barrier(jnp.sum(grad_queries, axis=0)), lax.optimization_barrier(jnp.sum(grad_values, axis=0))])
        grad_projected = jnp.concatenate([grad_queries, grad_keys, grad_values], axis=1).astype(jnp.bfloat16)
        grad_qkv = jnp.dot(normed_one.T, grad_projected, preferred_element_type=jnp.float32)
        grad_normed_one = jnp.dot(grad_projected, w_qkv.T, preferred_element_type=jnp.float32)
        grad_gain_one = lax.optimization_barrier(jnp.sum(grad_normed_one * scaled_one, axis=0))
        grad_shift_one = lax.optimization_barrier(jnp.sum(grad_normed_one, axis=0))
        grad_in = grad_residual + norm_backward(grad_normed_one, scaled_one, inverse_one, norm_one_gain)
        terms = (grad_gain_one, grad_shift_one, grad_qkv, grad_bias_qv, grad_out, grad_bias_out, grad_gain_two, grad_shift_two, grad_up, grad_bias_up, grad_down, grad_bias_down)
        new_totals = tuple((total + term for total, term in zip(totals, terms)))
        return (new_totals, (output, grad_in))
    start = (jnp.zeros((D,), jnp.float32), jnp.zeros((D,), jnp.float32), jnp.zeros((D, 3 * D), jnp.float32), jnp.zeros((2 * D,), jnp.float32), jnp.zeros((D, D), jnp.float32), jnp.zeros((D,), jnp.float32), jnp.zeros((D,), jnp.float32), jnp.zeros((D,), jnp.float32), jnp.zeros((D, FF), jnp.float32), jnp.zeros((FF,), jnp.float32), jnp.zeros((FF, D), jnp.float32), jnp.zeros((D,), jnp.float32))
    totals, stacked = lax.scan(one_sequence, start, (block_input, cotangent))
    outputs, grad_inputs = stacked
    scale = float(TOKENS) ** (-0.5)
    return (outputs, grad_inputs, totals[0] * scale, totals[1] * scale, totals[2] * scale, totals[3] * scale, totals[4] * scale, totals[5] * scale, totals[6] * scale, totals[7] * scale, totals[8] * scale, totals[9] * scale, totals[10] * scale, totals[11] * scale)
```

```python
import functools

import jax
import jax.numpy as jnp
from jax import lax
from jax.experimental import pallas as pl
from jax.experimental.pallas import tpu as pltpu
from jax.sharding import PartitionSpec as P

HEADS = 17
HEAD_DIM = 64


EPS = 1e-05
MASKED = -1e30
INV_ROOT_TWO = 0.7071067811865476
INV_ROOT_TWO_PI = 0.3989422804014327


def norm_forward(rows_in, gain, shift):
    center = jnp.mean(rows_in, axis=-1, keepdims=True)
    offset = rows_in - center
    spread = jnp.mean(offset * offset, axis=-1, keepdims=True)
    inverse = lax.rsqrt(spread + EPS)
    scaled = offset * inverse
    normed = (scaled * gain.astype(jnp.float32) + shift.astype(jnp.float32)).astype(jnp.bfloat16)
    return (scaled, inverse, normed)


def norm_backward(upstream, scaled, inverse, gain):
    weighted = upstream * gain.astype(jnp.float32)
    first = jnp.mean(weighted, axis=-1, keepdims=True)
    second = jnp.mean(weighted * scaled, axis=-1, keepdims=True)
    return inverse * (weighted - first - scaled * second)


def gelu_value(pre):
    return 0.5 * pre * (1.0 + lax.erf(pre * INV_ROOT_TWO))


def gelu_slope(pre):
    return (
        0.5 * (1.0 + lax.erf(pre * INV_ROOT_TWO))
        + pre * jnp.exp(-0.5 * pre * pre) * INV_ROOT_TWO_PI
    )


def inner_rows(left, right):
    return lax.dot_general(
        left, right, (((0,), (0,)), ((), ())), preferred_element_type=jnp.float32
    )


def outer_cols(left, right):
    return lax.dot_general(
        left, right, (((1,), (1,)), ((), ())), preferred_element_type=jnp.float32
    )


def head_view(block):
    return block.reshape(block.shape[0], block.shape[1], HEADS, HEAD_DIM)


def masked_scores(query_heads, key_heads, allowed, factor):
    scores = (
        jnp.einsum("sqhd,skhd->shqk", query_heads, key_heads, preferred_element_type=jnp.float32)
        * factor
    )
    return jnp.where(allowed, scores, MASKED)


def greet_all(count):
    me = lax.axis_index("ctx")
    barrier = pltpu.get_barrier_semaphore()
    for step in range(1, count):
        pl.semaphore_signal(
            barrier,
            inc=1,
            device_id={"ctx": lax.rem(me + step, count)},
            device_id_type=pl.DeviceIdType.MESH,
        )
    pl.semaphore_wait(barrier, count - 1)
    return me


def swap_kernel(count, in_ref, out_ref, send_sem, recv_sem):
    me = greet_all(count)
    copies = []
    for step in range(1, count):
        target = lax.rem(me + step, count)
        copy = pltpu.make_async_remote_copy(
            src_ref=in_ref.at[target],
            dst_ref=out_ref.at[me],
            send_sem=send_sem.at[step],
            recv_sem=recv_sem.at[step],
            device_id={"ctx": target},
            device_id_type=pl.DeviceIdType.MESH,
        )
        copy.start()
        copies.append(copy)
    out_ref[pl.ds(me, 1)] = in_ref[pl.ds(me, 1)]
    for copy in copies:
        copy.wait()


def share_kernel(count, in_ref, out_ref, send_sem, recv_sem):
    me = greet_all(count)
    copies = []
    for step in range(1, count):
        copy = pltpu.make_async_remote_copy(
            src_ref=in_ref,
            dst_ref=out_ref.at[me],
            send_sem=send_sem.at[step],
            recv_sem=recv_sem.at[step],
            device_id={"ctx": lax.rem(me + step, count)},
            device_id_type=pl.DeviceIdType.MESH,
        )
        copy.start()
        copies.append(copy)
    out_ref[pl.ds(me, 1)] = in_ref[...][None]
    for copy in copies:
        copy.wait()


def relay_kernel(count, in_ref, out_ref, send_sem, recv_sem):
    me = greet_all(count)
    partner = me + 1 - 2 * lax.rem(me, 2)
    across = lax.rem(me + 2, 4)

    def send(source, slot, sem, target):
        copy = pltpu.make_async_remote_copy(
            src_ref=source,
            dst_ref=out_ref.at[slot],
            send_sem=send_sem.at[sem],
            recv_sem=recv_sem.at[sem],
            device_id={"ctx": target},
            device_id_type=pl.DeviceIdType.MESH,
        )
        copy.start()
        return copy

    far = send(in_ref, me, 1, across)
    near = send(in_ref, me, 2, partner)
    out_ref[pl.ds(me, 1)] = in_ref[...][None]
    far.wait_recv()
    handed = send(out_ref.at[across], across, 3, partner)
    far.wait_send()
    near.wait()
    handed.wait()


def ctx_call(kernel, block, out_shape, ident):
    count = lax.axis_size("ctx")
    return pl.pallas_call(
        functools.partial(kernel, count),
        out_shape=jax.ShapeDtypeStruct(out_shape, block.dtype),
        in_specs=[pl.BlockSpec(memory_space=pltpu.VMEM)],
        out_specs=pl.BlockSpec(memory_space=pltpu.VMEM),
        scratch_shapes=[
            pltpu.SemaphoreType.DMA((count,)),
            pltpu.SemaphoreType.DMA((count,)),
        ],
        compiler_params=pltpu.CompilerParams(collective_id=ident, has_side_effects=True),
        name=f"ctx_exchange_{ident}",
    )(block)


def ctx_swap(block, ident):
    return ctx_call(swap_kernel, block, block.shape, ident)


def ctx_share(block, ident):
    count = lax.axis_size("ctx")
    kernel = relay_kernel if count == 4 else share_kernel
    return ctx_call(kernel, block, (count,) + block.shape, ident)


def on_device(
    block_input,
    norm_one_gain,
    norm_one_bias,
    w_qkv,
    bias_qv,
    w_out,
    bias_out,
    norm_two_gain,
    norm_two_bias,
    w_up,
    bias_up,
    w_down,
    bias_down,
    cotangent,
):
    low = jnp.bfloat16
    seq_count, block_len, width = block_input.shape
    rows = seq_count * block_len
    ctx = lax.axis_size("ctx")
    dp = lax.axis_size("dp")
    fold = dp // ctx
    me = lax.axis_index("ctx")
    seq_len = block_len * ctx
    tokens = rows * ctx
    grad_scale = float(tokens * dp) ** (-0.5)
    factor = float(HEAD_DIM) ** (-0.5)

    there = []
    for d in range(dp):
        for c in range(ctx):
            there.append((d * ctx + c, (fold * c + d % fold) * ctx + d // fold))
    back = [(b, a) for a, b in there]

    def columns_whole(piece):
        moved = lax.ppermute(piece, ("dp", "ctx"), there)
        whole = lax.all_gather(moved, "dp", axis=0, tiled=False)
        whole = whole.reshape(ctx, fold, piece.shape[0], piece.shape[1])
        return whole.transpose(0, 2, 1, 3).reshape(
            ctx * piece.shape[0], fold * piece.shape[1]
        )

    def columns_owned(part, piece):
        parts = part.reshape(ctx, piece.shape[0], fold, piece.shape[1]).transpose(0, 2, 1, 3)
        parts = parts.reshape(dp, piece.shape[0], piece.shape[1]).astype(low)
        mine = lax.psum_scatter(parts, "dp", scatter_dimension=0, tiled=False)
        return lax.ppermute(mine, ("dp", "ctx"), back).astype(jnp.float32) * grad_scale

    def rows_whole(piece):
        return lax.all_gather(piece.T, "dp", axis=0, tiled=True)

    def rows_owned(part):
        mine = lax.psum_scatter(part.astype(low), "dp", scatter_dimension=0, tiled=True)
        return mine.T.astype(jnp.float32) * grad_scale

    shards = (
        norm_one_gain,
        norm_one_bias,
        bias_qv,
        bias_out,
        norm_two_gain,
        norm_two_bias,
        bias_up,
        bias_down,
    )
    sizes = [v.shape[0] for v in shards]
    vectors = lax.all_gather(jnp.concatenate(shards), "dp", axis=0, tiled=False)
    full = []
    at = 0
    for size in sizes:
        full.append(vectors[:, at : at + size].reshape(dp * size).astype(jnp.float32))
        at += size
    (
        gain_one,
        shift_one,
        full_bias_qv,
        full_bias_out,
        gain_two,
        shift_two,
        full_bias_up,
        full_bias_down,
    ) = full

    qkv_c = columns_whole(w_qkv)
    out_c = rows_whole(w_out)
    up_c = columns_whole(w_up)
    down_c = rows_whole(w_down)

    inputs = block_input.reshape(rows, width).astype(jnp.float32)
    scaled_one, inverse_one, normed_one = norm_forward(inputs, gain_one, shift_one)
    normed_one_all = ctx_share(normed_one, 0).reshape(tokens, width)
    qkv_bias = jnp.concatenate(
        [full_bias_qv[:width], jnp.zeros((width,), jnp.float32), full_bias_qv[width:]]
    )
    span = qkv_c.shape[1]
    bias_c = lax.dynamic_slice_in_dim(qkv_bias, me * span, span)
    projected_c = (
        jnp.dot(normed_one_all, qkv_c, preferred_element_type=jnp.float32) + bias_c
    ).astype(low)
    projected = ctx_share(projected_c, 1)
    projected = (
        projected.reshape(ctx, ctx, seq_count, block_len, span)
        .transpose(2, 1, 3, 0, 4)
        .reshape(seq_count, seq_len, 3 * width)
    )
    queries = lax.dynamic_slice_in_dim(projected[:, :, :width], me * block_len, block_len, axis=1)
    query_heads = head_view(queries)
    key_heads = head_view(projected[:, :, width : 2 * width])
    value_heads = head_view(projected[:, :, 2 * width :])
    query_index = me * block_len + jnp.arange(block_len, dtype=jnp.int32)
    key_index = jnp.arange(seq_len, dtype=jnp.int32)
    allowed = key_index[None, :] <= query_index[:, None]
    scores = masked_scores(query_heads, key_heads, allowed, factor)
    peak = jnp.max(scores, axis=-1, keepdims=True)
    log_total = peak + jnp.log(jnp.sum(jnp.exp(scores - peak), axis=-1, keepdims=True))
    probs = jnp.exp(scores - log_total)
    soft_weights = probs.astype(low)
    mixed = jnp.einsum(
        "shqk,skhd->sqhd", soft_weights, value_heads, preferred_element_type=jnp.float32
    ).astype(low)

    slab = width // ctx

    def to_columns(block):
        wide = block.shape[1] // ctx
        swapped = block.reshape(rows, ctx, wide).transpose(1, 0, 2)
        return swapped

    mixed_c = ctx_swap(to_columns(mixed.reshape(rows, width)), 2).reshape(tokens, slab)
    out_part = outer_cols(mixed_c, out_c).astype(low).reshape(ctx, rows, width)
    out_sum = jnp.sum(ctx_swap(out_part, 3).astype(jnp.float32), axis=0)
    residual = inputs + (out_sum + full_bias_out)
    scaled_two, inverse_two, normed_two = norm_forward(residual, gain_two, shift_two)
    upstream = cotangent.reshape(rows, width)
    up_float = upstream.astype(jnp.float32)
    both = ctx_share(jnp.stack([normed_two, upstream]), 4)
    normed_two_all = both[:, 0].reshape(tokens, width)
    upstream_all = both[:, 1].reshape(tokens, width)
    units = up_c.shape[1]
    hidden_pre = jnp.dot(
        normed_two_all, up_c, preferred_element_type=jnp.float32
    ) + lax.dynamic_slice_in_dim(full_bias_up, me * units, units)
    hidden = gelu_value(hidden_pre).astype(low)
    down_part = outer_cols(hidden, down_c).astype(low).reshape(ctx, rows, width)
    grad_hidden = jnp.dot(
        upstream_all, down_c, preferred_element_type=jnp.float32
    ) * gelu_slope(hidden_pre)
    grad_hidden_low = grad_hidden.astype(low)
    normed_part = outer_cols(grad_hidden_low, up_c).astype(low).reshape(ctx, rows, width)
    sums = jnp.sum(
        ctx_swap(jnp.stack([down_part, normed_part], axis=1), 5).astype(jnp.float32), axis=0
    )
    block_output = (
        (residual + (sums[0] + full_bias_down)).astype(low).reshape(seq_count, block_len, width)
    )
    grad_normed_two = sums[1]
    grad_residual = up_float + norm_backward(grad_normed_two, scaled_two, inverse_two, gain_two)
    grad_residual_low = grad_residual.astype(low)
    grad_residual_all = ctx_share(grad_residual_low, 6).reshape(tokens, width)
    grad_mixed_c = jnp.dot(
        grad_residual_all, out_c, preferred_element_type=jnp.float32
    ).astype(low)
    grad_mixed = ctx_swap(grad_mixed_c.reshape(ctx, rows, slab), 7)
    grad_mixed = grad_mixed.transpose(1, 0, 2).reshape(seq_count, block_len, HEADS, HEAD_DIM)
    grad_probs = jnp.einsum(
        "sqhd,skhd->shqk", grad_mixed, value_heads, preferred_element_type=jnp.float32
    )
    delta = jnp.einsum("sqhd,sqhd->shq", grad_mixed, mixed, preferred_element_type=jnp.float32)[
        ..., None
    ]
    grad_scores = (probs * (grad_probs - delta) * factor).astype(low)
    grad_queries = jnp.einsum(
        "shqk,skhd->sqhd", grad_scores, key_heads, preferred_element_type=jnp.float32
    ).reshape(rows, width)
    key_part = jnp.einsum(
        "shqk,sqhd->skhd", grad_scores, query_heads, preferred_element_type=jnp.float32
    )
    value_part = jnp.einsum(
        "shqk,sqhd->skhd", soft_weights, grad_mixed, preferred_element_type=jnp.float32
    )

    def to_blocks(part):
        part = part.astype(low).reshape(seq_count, ctx, block_len, width)
        return part.transpose(1, 0, 2, 3).reshape(ctx, rows, width)

    pairs = jnp.stack([to_blocks(key_part), to_blocks(value_part)], axis=1)
    kv_sums = jnp.sum(ctx_swap(pairs, 8).astype(jnp.float32), axis=0)
    grad_keys, grad_values = kv_sums[0], kv_sums[1]
    grad_projected = jnp.concatenate([grad_queries, grad_keys, grad_values], axis=1).astype(low)
    grad_projected_c = ctx_swap(to_columns(grad_projected), 9).reshape(tokens, span)
    one_part = outer_cols(grad_projected_c, qkv_c).astype(low).reshape(ctx, rows, width)
    grad_normed_one = jnp.sum(ctx_swap(one_part, 10).astype(jnp.float32), axis=0)
    grad_input = grad_residual + norm_backward(grad_normed_one, scaled_one, inverse_one, gain_one)
    grad_input = grad_input.reshape(seq_count, block_len, width)

    grad_down = rows_owned(inner_rows(upstream_all, hidden))
    grad_up = columns_owned(inner_rows(normed_two_all, grad_hidden_low), w_up)
    grad_out = rows_owned(inner_rows(grad_residual_all, mixed_c))
    grad_qkv = columns_owned(inner_rows(normed_one_all, grad_projected_c), w_qkv)

    bias_up_c = jnp.sum(grad_hidden, axis=0)
    grad_bias_up = lax.dynamic_update_slice_in_dim(
        jnp.zeros((ctx * units,), jnp.float32), bias_up_c, me * units, axis=0
    )
    sums_here = (
        jnp.sum(grad_normed_one * scaled_one, axis=0),
        jnp.sum(grad_normed_one, axis=0),
        jnp.concatenate([jnp.sum(grad_queries, axis=0), jnp.sum(grad_values, axis=0)]),
        jnp.sum(grad_residual, axis=0),
        jnp.sum(grad_normed_two * scaled_two, axis=0),
        jnp.sum(grad_normed_two, axis=0),
        grad_bias_up,
        jnp.sum(up_float, axis=0),
    )
    table = jnp.concatenate([v.reshape(dp, -1) for v in sums_here], axis=1)
    table = jnp.sum(ctx_share(table, 11), axis=0)
    totals = lax.psum_scatter(table, "dp", scatter_dimension=0, tiled=False) * grad_scale
    owned = []
    at = 0
    for size in sizes:
        owned.append(totals[at : at + size])
        at += size
    return (
        block_output,
        grad_input,
        owned[0],
        owned[1],
        grad_qkv,
        owned[2],
        grad_out,
        owned[3],
        owned[4],
        owned[5],
        grad_up,
        owned[6],
        grad_down,
        owned[7],
    )


def solution(mesh):
    in_specs = (
        P("dp", "ctx", None),
        P("dp"),
        P("dp"),
        P("ctx", "dp"),
        P("dp"),
        P("ctx", "dp"),
        P("dp"),
        P("dp"),
        P("dp"),
        P("ctx", "dp"),
        P("dp"),
        P("ctx", "dp"),
        P("dp"),
        P("dp", "ctx", None),
    )
    out_specs = (
        P("dp", "ctx", None),
        P("dp", "ctx", None),
        P("dp"),
        P("dp"),
        P("ctx", "dp"),
        P("dp"),
        P("ctx", "dp"),
        P("dp"),
        P("dp"),
        P("dp"),
        P("ctx", "dp"),
        P("dp"),
        P("ctx", "dp"),
        P("dp"),
    )
    return jax.shard_map(
        on_device, mesh=mesh, in_specs=in_specs, out_specs=out_specs, check_vma=False
    )
```

```python
import functools

import jax
import jax.numpy as jnp
from jax import lax
from jax.experimental import pallas as pl
from jax.experimental.pallas import tpu as pltpu
from jax.sharding import PartitionSpec as P

HEADS = 17
HEAD_DIM = 64


EPS = 1e-05
MASKED = -1e30
INV_ROOT_TWO = 0.7071067811865476
INV_ROOT_TWO_PI = 0.3989422804014327


def norm_forward(rows_in, gain, shift):
    center = jnp.mean(rows_in, axis=-1, keepdims=True)
    offset = rows_in - center
    spread = jnp.mean(offset * offset, axis=-1, keepdims=True)
    inverse = lax.rsqrt(spread + EPS)
    scaled = offset * inverse
    normed = (scaled * gain.astype(jnp.float32) + shift.astype(jnp.float32)).astype(jnp.bfloat16)
    return (scaled, inverse, normed)


def norm_backward(upstream, scaled, inverse, gain):
    weighted = upstream * gain.astype(jnp.float32)
    first = jnp.mean(weighted, axis=-1, keepdims=True)
    second = jnp.mean(weighted * scaled, axis=-1, keepdims=True)
    return inverse * (weighted - first - scaled * second)


def gelu_value(pre):
    return 0.5 * pre * (1.0 + lax.erf(pre * INV_ROOT_TWO))


def gelu_slope(pre):
    return (
        0.5 * (1.0 + lax.erf(pre * INV_ROOT_TWO))
        + pre * jnp.exp(-0.5 * pre * pre) * INV_ROOT_TWO_PI
    )


def inner_rows(left, right):
    return lax.dot_general(
        left, right, (((0,), (0,)), ((), ())), preferred_element_type=jnp.float32
    )


def outer_cols(left, right):
    return lax.dot_general(
        left, right, (((1,), (1,)), ((), ())), preferred_element_type=jnp.float32
    )


def head_view(block):
    return block.reshape(block.shape[0], block.shape[1], HEADS, HEAD_DIM)


def masked_scores(query_heads, key_heads, allowed, factor):
    scores = (
        jnp.einsum("sqhd,skhd->shqk", query_heads, key_heads, preferred_element_type=jnp.float32)
        * factor
    )
    return jnp.where(allowed, scores, MASKED)


def greet_all(count):
    me = lax.axis_index("ctx")
    barrier = pltpu.get_barrier_semaphore()
    for step in range(1, count):
        pl.semaphore_signal(
            barrier,
            inc=1,
            device_id={"ctx": lax.rem(me + step, count)},
            device_id_type=pl.DeviceIdType.MESH,
        )
    pl.semaphore_wait(barrier, count - 1)
    return me


def swap_kernel(count, in_ref, out_ref, send_sem, recv_sem):
    me = greet_all(count)
    copies = []
    for step in range(1, count):
        target = lax.rem(me + step, count)
        copy = pltpu.make_async_remote_copy(
            src_ref=in_ref.at[target],
            dst_ref=out_ref.at[me],
            send_sem=send_sem.at[step],
            recv_sem=recv_sem.at[step],
            device_id={"ctx": target},
            device_id_type=pl.DeviceIdType.MESH,
        )
        copy.start()
        copies.append(copy)
    out_ref[pl.ds(me, 1)] = in_ref[pl.ds(me, 1)]
    for copy in copies:
        copy.wait()


def share_kernel(count, in_ref, out_ref, send_sem, recv_sem):
    me = greet_all(count)
    copies = []
    for step in range(1, count):
        copy = pltpu.make_async_remote_copy(
            src_ref=in_ref,
            dst_ref=out_ref.at[me],
            send_sem=send_sem.at[step],
            recv_sem=recv_sem.at[step],
            device_id={"ctx": lax.rem(me + step, count)},
            device_id_type=pl.DeviceIdType.MESH,
        )
        copy.start()
        copies.append(copy)
    out_ref[pl.ds(me, 1)] = in_ref[...][None]
    for copy in copies:
        copy.wait()


def relay_kernel(count, in_ref, out_ref, send_sem, recv_sem):
    me = greet_all(count)
    partner = me + 1 - 2 * lax.rem(me, 2)
    across = lax.rem(me + 2, 4)

    def send(source, slot, sem, target):
        copy = pltpu.make_async_remote_copy(
            src_ref=source,
            dst_ref=out_ref.at[slot],
            send_sem=send_sem.at[sem],
            recv_sem=recv_sem.at[sem],
            device_id={"ctx": target},
            device_id_type=pl.DeviceIdType.MESH,
        )
        copy.start()
        return copy

    far = send(in_ref, me, 1, across)
    near = send(in_ref, me, 2, partner)
    out_ref[pl.ds(me, 1)] = in_ref[...][None]
    far.wait_recv()
    handed = send(out_ref.at[across], across, 3, partner)
    far.wait_send()
    near.wait()
    handed.wait()


def ctx_call(kernel, block, out_shape, ident):
    count = lax.axis_size("ctx")
    return pl.pallas_call(
        functools.partial(kernel, count),
        out_shape=jax.ShapeDtypeStruct(out_shape, block.dtype),
        in_specs=[pl.BlockSpec(memory_space=pltpu.VMEM)],
        out_specs=pl.BlockSpec(memory_space=pltpu.VMEM),
        scratch_shapes=[
            pltpu.SemaphoreType.DMA((count,)),
            pltpu.SemaphoreType.DMA((count,)),
        ],
        compiler_params=pltpu.CompilerParams(collective_id=ident, has_side_effects=True),
        name=f"ctx_exchange_{ident}",
    )(block)


def ctx_swap(block, ident):
    return ctx_call(swap_kernel, block, block.shape, ident)


def ctx_share(block, ident):
    count = lax.axis_size("ctx")
    kernel = relay_kernel if count == 4 else share_kernel
    return ctx_call(kernel, block, (count,) + block.shape, ident)


def owners_kernel(count, *refs):
    arrays = (len(refs) - 2) // 2
    sources, results = refs[:arrays], refs[arrays : 2 * arrays]
    send_sem, recv_sem = refs[2 * arrays :]
    me = lax.axis_index("dp")
    barrier = pltpu.get_barrier_semaphore()
    for step in range(1, count):
        pl.semaphore_signal(
            barrier,
            inc=1,
            device_id={"dp": lax.rem(me + step, count)},
            device_id_type=pl.DeviceIdType.MESH,
        )
    pl.semaphore_wait(barrier, count - 1)

    def copy_of(step, which):
        target = lax.rem(me + step, count)
        return pltpu.make_async_remote_copy(
            src_ref=sources[which].at[target],
            dst_ref=results[which].at[me],
            send_sem=send_sem.at[which, step],
            recv_sem=recv_sem.at[which, step],
            device_id={"dp": target},
            device_id_type=pl.DeviceIdType.MESH,
        )

    def start(step, carry):
        for which in range(arrays):
            copy_of(step, which).start()
        return carry

    def finish(step, carry):
        for which in range(arrays):
            copy_of(step, which).wait()
        return carry

    lax.fori_loop(1, count, start, 0)
    for which in range(arrays):
        results[which][pl.ds(me, 1)] = sources[which][pl.ds(me, 1)]
    lax.fori_loop(1, count, finish, 0)


def to_owners(arrays, ident):
    count = lax.axis_size("dp")
    return pl.pallas_call(
        functools.partial(owners_kernel, count),
        out_shape=[jax.ShapeDtypeStruct(a.shape, a.dtype) for a in arrays],
        in_specs=[pl.BlockSpec(memory_space=pltpu.VMEM)] * len(arrays),
        out_specs=[pl.BlockSpec(memory_space=pltpu.VMEM)] * len(arrays),
        scratch_shapes=[
            pltpu.SemaphoreType.DMA((len(arrays), count)),
            pltpu.SemaphoreType.DMA((len(arrays), count)),
        ],
        compiler_params=pltpu.CompilerParams(collective_id=ident, has_side_effects=True),
        name=f"dp_owners_{ident}",
    )(*arrays)


def on_device(
    block_input,
    norm_one_gain,
    norm_one_bias,
    w_qkv,
    bias_qv,
    w_out,
    bias_out,
    norm_two_gain,
    norm_two_bias,
    w_up,
    bias_up,
    w_down,
    bias_down,
    cotangent,
):
    low = jnp.bfloat16
    seq_count, block_len, width = block_input.shape
    rows = seq_count * block_len
    ctx = lax.axis_size("ctx")
    dp = lax.axis_size("dp")
    fold = dp // ctx
    me = lax.axis_index("ctx")
    seq_len = block_len * ctx
    tokens = rows * ctx
    grad_scale = float(tokens * dp) ** (-0.5)
    factor = float(HEAD_DIM) ** (-0.5)

    there = []
    for d in range(dp):
        for c in range(ctx):
            there.append((d * ctx + c, (fold * c + d % fold) * ctx + d // fold))
    back = [(b, a) for a, b in there]

    def columns_joined(whole):
        high, wide = whole.shape[1:]
        whole = whole.reshape(ctx, fold, high, wide)
        return whole.transpose(0, 2, 1, 3).reshape(ctx * high, fold * wide)

    def columns_whole(piece):
        moved = lax.ppermute(piece, ("dp", "ctx"), there)
        return columns_joined(lax.all_gather(moved, "dp", axis=0, tiled=False))

    def columns_split(part, piece):
        parts = part.reshape(ctx, piece.shape[0], fold, piece.shape[1]).transpose(0, 2, 1, 3)
        return parts.reshape(dp, piece.shape[0], piece.shape[1]).astype(low)

    def columns_back(mine):
        return lax.ppermute(mine.astype(low), ("dp", "ctx"), back).astype(jnp.float32) * grad_scale

    def rows_whole(piece):
        return lax.all_gather(piece.T, "dp", axis=0, tiled=True)

    shards = (
        norm_one_gain,
        norm_one_bias,
        bias_qv,
        bias_out,
        norm_two_gain,
        norm_two_bias,
        bias_up,
        bias_down,
    )
    sizes = [v.shape[0] for v in shards]
    lanes = w_qkv.shape[1] + w_out.shape[1]
    packed = jnp.concatenate(shards)
    used = packed.shape[0]
    packed = jnp.pad(packed, (0, -used % lanes)).reshape(-1, lanes)
    moved_qkv = lax.ppermute(w_qkv, ("dp", "ctx"), there)
    first = jnp.concatenate([jnp.concatenate([moved_qkv, w_out], axis=1), packed], axis=0)
    first = lax.all_gather(first, "dp", axis=0, tiled=False)
    part_rows, part_cols = w_qkv.shape
    vectors = first[:, part_rows:].reshape(dp, -1)[:, :used]
    full = []
    at = 0
    for size in sizes:
        full.append(vectors[:, at : at + size].reshape(dp * size).astype(jnp.float32))
        at += size
    (
        gain_one,
        shift_one,
        full_bias_qv,
        full_bias_out,
        gain_two,
        shift_two,
        full_bias_up,
        full_bias_down,
    ) = full

    qkv_c = columns_joined(first[:, :part_rows, :part_cols])
    out_c = (
        first[:, :part_rows, part_cols:].transpose(1, 0, 2).reshape(part_rows, dp * w_out.shape[1])
    )
    up_c = columns_whole(w_up)
    down_c = rows_whole(w_down)

    inputs = block_input.reshape(rows, width).astype(jnp.float32)
    scaled_one, inverse_one, _ = norm_forward(inputs, gain_one, shift_one)
    upstream = cotangent.reshape(rows, width)
    both = ctx_share(jnp.stack([block_input.reshape(rows, width), upstream]), 0)
    upstream_all = both[:, 1].reshape(tokens, width)
    inputs_all = both[:, 0].reshape(tokens, width).astype(jnp.float32)
    normed_one_all = norm_forward(inputs_all, gain_one, shift_one)[2]
    qkv_bias = jnp.concatenate(
        [full_bias_qv[:width], jnp.zeros((width,), jnp.float32), full_bias_qv[width:]]
    )
    span = qkv_c.shape[1]
    bias_c = lax.dynamic_slice_in_dim(qkv_bias, me * span, span)
    projected_c = (
        jnp.dot(normed_one_all, qkv_c, preferred_element_type=jnp.float32) + bias_c
    ).astype(low)
    projected = ctx_share(projected_c, 1)
    projected = (
        projected.reshape(ctx, ctx, seq_count, block_len, span)
        .transpose(2, 1, 3, 0, 4)
        .reshape(seq_count, seq_len, 3 * width)
    )
    queries = lax.dynamic_slice_in_dim(projected[:, :, :width], me * block_len, block_len, axis=1)
    query_heads = head_view(queries)
    key_heads = head_view(projected[:, :, width : 2 * width])
    value_heads = head_view(projected[:, :, 2 * width :])
    query_index = me * block_len + jnp.arange(block_len, dtype=jnp.int32)
    key_index = jnp.arange(seq_len, dtype=jnp.int32)
    allowed = key_index[None, :] <= query_index[:, None]
    scores = masked_scores(query_heads, key_heads, allowed, factor)
    peak = jnp.max(scores, axis=-1, keepdims=True)
    log_total = peak + jnp.log(jnp.sum(jnp.exp(scores - peak), axis=-1, keepdims=True))
    probs = jnp.exp(scores - log_total)
    soft_weights = probs.astype(low)
    mixed = jnp.einsum(
        "shqk,skhd->sqhd", soft_weights, value_heads, preferred_element_type=jnp.float32
    ).astype(low)

    slab = width // ctx

    def to_columns(block):
        wide = block.shape[1] // ctx
        swapped = block.reshape(rows, ctx, wide).transpose(1, 0, 2)
        return swapped

    mixed_c = ctx_swap(to_columns(mixed.reshape(rows, width)), 2).reshape(tokens, slab)
    out_part = jnp.dot(mixed_c, out_c, preferred_element_type=jnp.float32).astype(low).reshape(ctx, rows, width)
    out_sum = jnp.sum(ctx_swap(out_part, 3).astype(jnp.float32), axis=0)
    residual = inputs + (out_sum + full_bias_out)
    scaled_two, inverse_two, normed_two = norm_forward(residual, gain_two, shift_two)
    up_float = upstream.astype(jnp.float32)
    normed_two_all = ctx_share(normed_two, 4).reshape(tokens, width)
    units = up_c.shape[1]
    hidden_pre = jnp.dot(
        normed_two_all, up_c, preferred_element_type=jnp.float32
    ) + lax.dynamic_slice_in_dim(full_bias_up, me * units, units)
    hidden = gelu_value(hidden_pre).astype(low)
    down_part = outer_cols(hidden, down_c).astype(low).reshape(ctx, rows, width)
    grad_hidden = jnp.dot(
        upstream_all, down_c, preferred_element_type=jnp.float32
    ) * gelu_slope(hidden_pre)
    grad_hidden_low = grad_hidden.astype(low)
    normed_part = outer_cols(grad_hidden_low, up_c).astype(low).reshape(ctx, rows, width)
    sums = jnp.sum(
        ctx_swap(jnp.stack([down_part, normed_part], axis=1), 5).astype(jnp.float32), axis=0
    )
    down_grad = inner_rows(upstream_all, hidden).astype(low)
    up_grad = columns_split(inner_rows(normed_two_all, grad_hidden_low), w_up)
    down_grad, up_grad, sums = lax.optimization_barrier((down_grad, up_grad, sums))
    down_mine = lax.psum_scatter(down_grad, "dp", scatter_dimension=0, tiled=True)
    up_mine = lax.psum_scatter(up_grad, "dp", scatter_dimension=0, tiled=False)
    block_output = (
        (residual + (sums[0] + full_bias_down)).astype(low).reshape(seq_count, block_len, width)
    )
    grad_normed_two = sums[1]
    grad_residual = up_float + norm_backward(grad_normed_two, scaled_two, inverse_two, gain_two)
    grad_residual_low = grad_residual.astype(low)
    grad_residual_all = ctx_share(grad_residual_low, 6).reshape(tokens, width)
    grad_mixed_c = outer_cols(grad_residual_all, out_c).astype(low)
    grad_mixed = ctx_swap(grad_mixed_c.reshape(ctx, rows, slab), 7)
    grad_mixed = grad_mixed.transpose(1, 0, 2).reshape(seq_count, block_len, HEADS, HEAD_DIM)
    grad_probs = jnp.einsum(
        "sqhd,skhd->shqk", grad_mixed, value_heads, preferred_element_type=jnp.float32
    )
    delta = jnp.einsum("sqhd,sqhd->shq", grad_mixed, mixed, preferred_element_type=jnp.float32)[
        ..., None
    ]
    grad_scores = (probs * (grad_probs - delta) * factor).astype(low)
    grad_queries = jnp.einsum(
        "shqk,skhd->sqhd", grad_scores, key_heads, preferred_element_type=jnp.float32
    ).reshape(rows, width)
    key_part = jnp.einsum(
        "shqk,sqhd->skhd", grad_scores, query_heads, preferred_element_type=jnp.float32
    )
    value_part = jnp.einsum(
        "shqk,sqhd->skhd", soft_weights, grad_mixed, preferred_element_type=jnp.float32
    )

    def to_blocks(part):
        part = part.astype(low).reshape(seq_count, ctx, block_len, width)
        return part.transpose(1, 0, 2, 3).reshape(ctx, rows, width)

    pairs = jnp.stack([to_blocks(key_part), to_blocks(value_part)], axis=1)
    kv_sums = jnp.sum(ctx_swap(pairs, 8).astype(jnp.float32), axis=0)
    grad_keys, grad_values = kv_sums[0], kv_sums[1]
    grad_projected = jnp.concatenate([grad_queries, grad_keys, grad_values], axis=1).astype(low)
    grad_projected_c = ctx_swap(to_columns(grad_projected), 9).reshape(tokens, span)
    one_part = outer_cols(grad_projected_c, qkv_c).astype(low).reshape(ctx, rows, width)
    grad_normed_one = jnp.sum(ctx_swap(one_part, 10).astype(jnp.float32), axis=0)
    grad_input = grad_residual + norm_backward(grad_normed_one, scaled_one, inverse_one, gain_one)
    grad_input = grad_input.reshape(seq_count, block_len, width)

    grad_down = down_mine.T.astype(jnp.float32) * grad_scale
    grad_up = columns_back(up_mine)
    qkv_parts = columns_split(inner_rows(normed_one_all, grad_projected_c), w_qkv)
    out_parts = (
        inner_rows(grad_residual_all, mixed_c).astype(low).reshape(dp, w_out.shape[1], slab)
    )

    bias_up_c = jnp.sum(grad_hidden, axis=0)
    grad_bias_up = lax.dynamic_update_slice_in_dim(
        jnp.zeros((ctx * units,), jnp.float32), bias_up_c, me * units, axis=0
    )
    sums_here = (
        jnp.sum(grad_normed_one * scaled_one, axis=0),
        jnp.sum(grad_normed_one, axis=0),
        jnp.concatenate([jnp.sum(grad_queries, axis=0), jnp.sum(grad_values, axis=0)]),
        jnp.sum(grad_residual, axis=0),
        jnp.sum(grad_normed_two * scaled_two, axis=0),
        jnp.sum(grad_normed_two, axis=0),
        grad_bias_up,
        jnp.sum(up_float, axis=0),
    )
    table = jnp.concatenate([v.reshape(dp, -1) for v in sums_here], axis=1)
    table = jnp.sum(ctx_share(table, 11), axis=0)
    qkv_parts, out_parts, table = to_owners([qkv_parts, out_parts, table[:, None]], 12)
    grad_qkv = columns_back(jnp.sum(qkv_parts.astype(jnp.float32), axis=0))
    grad_out = jnp.sum(out_parts.astype(jnp.float32), axis=0).T * grad_scale
    totals = jnp.sum(table, axis=(0, 1)) * grad_scale
    owned = []
    at = 0
    for size in sizes:
        owned.append(totals[at : at + size])
        at += size
    return (
        block_output,
        grad_input,
        owned[0],
        owned[1],
        grad_qkv,
        owned[2],
        grad_out,
        owned[3],
        owned[4],
        owned[5],
        grad_up,
        owned[6],
        grad_down,
        owned[7],
    )


def solution(mesh):
    in_specs = (
        P("dp", "ctx", None),
        P("dp"),
        P("dp"),
        P("ctx", "dp"),
        P("dp"),
        P("ctx", "dp"),
        P("dp"),
        P("dp"),
        P("dp"),
        P("ctx", "dp"),
        P("dp"),
        P("ctx", "dp"),
        P("dp"),
        P("dp", "ctx", None),
    )
    out_specs = (
        P("dp", "ctx", None),
        P("dp", "ctx", None),
        P("dp"),
        P("dp"),
        P("ctx", "dp"),
        P("dp"),
        P("ctx", "dp"),
        P("dp"),
        P("dp"),
        P("dp"),
        P("ctx", "dp"),
        P("dp"),
        P("ctx", "dp"),
        P("dp"),
    )
    return jax.shard_map(
        on_device, mesh=mesh, in_specs=in_specs, out_specs=out_specs, check_vma=False
    )
```

```python
import functools

import jax
import jax.numpy as jnp
from jax import lax
from jax.experimental import pallas as pl
from jax.experimental.pallas import tpu as pltpu
from jax.sharding import PartitionSpec as P

HEADS = 17
HEAD_DIM = 64


EPS = 1e-05
MASKED = -1e30
INV_ROOT_TWO = 0.7071067811865476
INV_ROOT_TWO_PI = 0.3989422804014327


def norm_forward(rows_in, gain, shift):
    center = jnp.mean(rows_in, axis=-1, keepdims=True)
    offset = rows_in - center
    spread = jnp.mean(offset * offset, axis=-1, keepdims=True)
    inverse = lax.rsqrt(spread + EPS)
    scaled = offset * inverse
    normed = (scaled * gain.astype(jnp.float32) + shift.astype(jnp.float32)).astype(jnp.bfloat16)
    return (scaled, inverse, normed)


def norm_backward(upstream, scaled, inverse, gain):
    weighted = upstream * gain.astype(jnp.float32)
    first = jnp.mean(weighted, axis=-1, keepdims=True)
    second = jnp.mean(weighted * scaled, axis=-1, keepdims=True)
    return inverse * (weighted - first - scaled * second)


def gelu_value(pre):
    return 0.5 * pre * (1.0 + lax.erf(pre * INV_ROOT_TWO))


def gelu_slope(pre):
    return (
        0.5 * (1.0 + lax.erf(pre * INV_ROOT_TWO))
        + pre * jnp.exp(-0.5 * pre * pre) * INV_ROOT_TWO_PI
    )


def inner_rows(left, right):
    return lax.dot_general(
        left, right, (((0,), (0,)), ((), ())), preferred_element_type=jnp.float32
    )


def outer_cols(left, right):
    return lax.dot_general(
        left, right, (((1,), (1,)), ((), ())), preferred_element_type=jnp.float32
    )


def head_view(block):
    return block.reshape(block.shape[0], block.shape[1], HEADS, HEAD_DIM)


def masked_scores(query_heads, key_heads, allowed, factor):
    scores = (
        jnp.einsum("sqhd,skhd->shqk", query_heads, key_heads, preferred_element_type=jnp.float32)
        * factor
    )
    return jnp.where(allowed, scores, MASKED)


def greet_all(count):
    me = lax.axis_index("ctx")
    barrier = pltpu.get_barrier_semaphore()
    for step in range(1, count):
        pl.semaphore_signal(
            barrier,
            inc=1,
            device_id={"ctx": lax.rem(me + step, count)},
            device_id_type=pl.DeviceIdType.MESH,
        )
    pl.semaphore_wait(barrier, count - 1)
    return me


def swap_kernel(count, in_ref, out_ref, send_sem, recv_sem):
    me = greet_all(count)
    copies = []
    for step in range(1, count):
        target = lax.rem(me + step, count)
        copy = pltpu.make_async_remote_copy(
            src_ref=in_ref.at[target],
            dst_ref=out_ref.at[me],
            send_sem=send_sem.at[step],
            recv_sem=recv_sem.at[step],
            device_id={"ctx": target},
            device_id_type=pl.DeviceIdType.MESH,
        )
        copy.start()
        copies.append(copy)
    out_ref[pl.ds(me, 1)] = in_ref[pl.ds(me, 1)]
    for copy in copies:
        copy.wait()


def share_kernel(count, in_ref, out_ref, send_sem, recv_sem):
    me = greet_all(count)
    copies = []
    for step in range(1, count):
        copy = pltpu.make_async_remote_copy(
            src_ref=in_ref,
            dst_ref=out_ref.at[me],
            send_sem=send_sem.at[step],
            recv_sem=recv_sem.at[step],
            device_id={"ctx": lax.rem(me + step, count)},
            device_id_type=pl.DeviceIdType.MESH,
        )
        copy.start()
        copies.append(copy)
    out_ref[pl.ds(me, 1)] = in_ref[...][None]
    for copy in copies:
        copy.wait()


def relay_kernel(count, in_ref, out_ref, send_sem, recv_sem):
    me = greet_all(count)
    partner = me + 1 - 2 * lax.rem(me, 2)
    across = lax.rem(me + 2, 4)

    chunks = send_sem.shape[1]
    size = in_ref.shape[0] // chunks

    def send(source, slot, sem, part, target):
        copy = pltpu.make_async_remote_copy(
            src_ref=source,
            dst_ref=out_ref.at[slot, pl.ds(part * size, size)],
            send_sem=send_sem.at[sem, part],
            recv_sem=recv_sem.at[sem, part],
            device_id={"ctx": target},
            device_id_type=pl.DeviceIdType.MESH,
        )
        copy.start()
        return copy

    mine = [in_ref.at[pl.ds(part * size, size)] for part in range(chunks)]
    far = [send(mine[part], me, 0, part, across) for part in range(chunks)]
    near = [send(mine[part], me, 1, part, partner) for part in range(chunks)]
    out_ref[pl.ds(me, 1)] = in_ref[...][None]
    handed = []
    for part in range(chunks):
        far[part].wait_recv()
        landed = out_ref.at[across, pl.ds(part * size, size)]
        handed.append(send(landed, across, 2, part, partner))
    for part in range(chunks):
        far[part].wait_send()
        near[part].wait()
        handed[part].wait()


def fold_kernel(count, in_ref, out_ref, near_in, held, far_in, send_sem, recv_sem):
    me = greet_all(count)
    even = lax.rem(me, 2)
    partner = me + 1 - 2 * even
    across = lax.rem(me + 2, 4)
    corner = lax.rem(partner + 2, 4)
    chunks = send_sem.shape[1]
    size = in_ref.shape[1] // chunks

    def send(source, dest, sem, part, target):
        copy = pltpu.make_async_remote_copy(
            src_ref=source,
            dst_ref=dest,
            send_sem=send_sem.at[sem, part],
            recv_sem=recv_sem.at[sem, part],
            device_id={"ctx": target},
            device_id_type=pl.DeviceIdType.MESH,
        )
        copy.start()
        return copy

    spans = [pl.ds(part * size, size) for part in range(chunks)]
    first = [
        send(in_ref.at[corner, s], near_in.at[0, s], 0, part, partner)
        for part, s in enumerate(spans)
    ]
    own = [
        send(in_ref.at[partner, s], near_in.at[1, s], 1, part, partner)
        for part, s in enumerate(spans)
    ]
    far = []
    for part, s in enumerate(spans):
        first[part].wait_recv()
        held[s] = (
            in_ref[across, s].astype(jnp.float32) + near_in[0, s].astype(jnp.float32)
        ).astype(held.dtype)
        far.append(send(held.at[s], far_in.at[s], 2, part, across))
    for part, s in enumerate(spans):
        own[part].wait_recv()
        out_ref[s] = in_ref[me, s].astype(jnp.float32) + near_in[1, s].astype(jnp.float32)
    for part, s in enumerate(spans):
        far[part].wait_recv()
        out_ref[s] = out_ref[s] + far_in[s].astype(jnp.float32)
    for part in range(chunks):
        first[part].wait_send()
        own[part].wait_send()
        far[part].wait_send()


def chunk_count(rows):
    return 4 if rows % 64 == 0 else 1


def ctx_call(kernel, block, out_shape, ident, out_dtype=None, chunks=1, scratch=()):
    count = lax.axis_size("ctx")
    return pl.pallas_call(
        functools.partial(kernel, count),
        out_shape=jax.ShapeDtypeStruct(out_shape, out_dtype or block.dtype),
        in_specs=[pl.BlockSpec(memory_space=pltpu.VMEM)],
        out_specs=pl.BlockSpec(memory_space=pltpu.VMEM),
        scratch_shapes=[
            *scratch,
            pltpu.SemaphoreType.DMA((count, chunks) if chunks else (count,)),
            pltpu.SemaphoreType.DMA((count, chunks) if chunks else (count,)),
        ],
        compiler_params=pltpu.CompilerParams(collective_id=ident, has_side_effects=True),
        name=f"ctx_exchange_{ident}",
    )(block)


def ctx_swap(block, ident):
    return ctx_call(swap_kernel, block, block.shape, ident, chunks=0)


def ctx_share(block, ident):
    count = lax.axis_size("ctx")
    if count != 4:
        return ctx_call(share_kernel, block, (count,) + block.shape, ident, chunks=0)
    flat = block.reshape(-1, block.shape[-1])
    whole = ctx_call(
        relay_kernel, flat, (count,) + flat.shape, ident, chunks=chunk_count(flat.shape[0])
    )
    return whole.reshape((count,) + block.shape)


def ctx_sum(block, ident):
    count = lax.axis_size("ctx")
    if count != 4:
        return jnp.sum(ctx_swap(block, ident).astype(jnp.float32), axis=0)
    shape = block.shape[1:]
    flat = block.reshape(count, -1, shape[-1])
    rows, wide = flat.shape[1:]
    total = ctx_call(
        fold_kernel,
        flat,
        (rows, wide),
        ident,
        out_dtype=jnp.float32,
        chunks=chunk_count(rows),
        scratch=(
            pltpu.VMEM((2, rows, wide), block.dtype),
            pltpu.VMEM((rows, wide), block.dtype),
            pltpu.VMEM((rows, wide), block.dtype),
        ),
    )
    return total.reshape(shape)


def owners_kernel(count, *refs):
    arrays = (len(refs) - 2) // 2
    sources, results = refs[:arrays], refs[arrays : 2 * arrays]
    send_sem, recv_sem = refs[2 * arrays :]
    me = lax.axis_index("dp")
    barrier = pltpu.get_barrier_semaphore()
    for step in range(1, count):
        pl.semaphore_signal(
            barrier,
            inc=1,
            device_id={"dp": lax.rem(me + step, count)},
            device_id_type=pl.DeviceIdType.MESH,
        )
    pl.semaphore_wait(barrier, count - 1)

    def copy_of(step, which):
        target = lax.rem(me + step, count)
        return pltpu.make_async_remote_copy(
            src_ref=sources[which].at[target],
            dst_ref=results[which].at[me],
            send_sem=send_sem.at[which, step],
            recv_sem=recv_sem.at[which, step],
            device_id={"dp": target},
            device_id_type=pl.DeviceIdType.MESH,
        )

    def start(step, carry):
        for which in range(arrays):
            copy_of(step, which).start()
        return carry

    def finish(step, carry):
        for which in range(arrays):
            copy_of(step, which).wait()
        return carry

    lax.fori_loop(1, count, start, 0)
    for which in range(arrays):
        results[which][pl.ds(me, 1)] = sources[which][pl.ds(me, 1)]
    lax.fori_loop(1, count, finish, 0)


def to_owners(arrays, ident):
    count = lax.axis_size("dp")
    return pl.pallas_call(
        functools.partial(owners_kernel, count),
        out_shape=[jax.ShapeDtypeStruct(a.shape, a.dtype) for a in arrays],
        in_specs=[pl.BlockSpec(memory_space=pltpu.VMEM)] * len(arrays),
        out_specs=[pl.BlockSpec(memory_space=pltpu.VMEM)] * len(arrays),
        scratch_shapes=[
            pltpu.SemaphoreType.DMA((len(arrays), count)),
            pltpu.SemaphoreType.DMA((len(arrays), count)),
        ],
        compiler_params=pltpu.CompilerParams(collective_id=ident, has_side_effects=True),
        name=f"dp_owners_{ident}",
    )(*arrays)


def on_device(
    block_input,
    norm_one_gain,
    norm_one_bias,
    w_qkv,
    bias_qv,
    w_out,
    bias_out,
    norm_two_gain,
    norm_two_bias,
    w_up,
    bias_up,
    w_down,
    bias_down,
    cotangent,
):
    low = jnp.bfloat16
    seq_count, block_len, width = block_input.shape
    rows = seq_count * block_len
    ctx = lax.axis_size("ctx")
    dp = lax.axis_size("dp")
    fold = dp // ctx
    me = lax.axis_index("ctx")
    seq_len = block_len * ctx
    tokens = rows * ctx
    grad_scale = float(tokens * dp) ** (-0.5)
    factor = float(HEAD_DIM) ** (-0.5)

    there = []
    for d in range(dp):
        for c in range(ctx):
            there.append((d * ctx + c, (fold * c + d % fold) * ctx + d // fold))
    back = [(b, a) for a, b in there]

    def columns_joined(whole):
        high, wide = whole.shape[1:]
        whole = whole.reshape(ctx, fold, high, wide)
        return whole.transpose(0, 2, 1, 3).reshape(ctx * high, fold * wide)

    def columns_whole(piece):
        moved = lax.ppermute(piece, ("dp", "ctx"), there)
        return columns_joined(lax.all_gather(moved, "dp", axis=0, tiled=False))

    def columns_split(part, piece):
        parts = part.reshape(ctx, piece.shape[0], fold, piece.shape[1]).transpose(0, 2, 1, 3)
        return parts.reshape(dp, piece.shape[0], piece.shape[1]).astype(low)

    def columns_back(mine):
        return lax.ppermute(mine.astype(low), ("dp", "ctx"), back).astype(jnp.float32) * grad_scale

    def rows_whole(piece):
        return lax.all_gather(piece.T, "dp", axis=0, tiled=True)

    shards = (
        norm_one_gain,
        norm_one_bias,
        bias_qv,
        bias_out,
        norm_two_gain,
        norm_two_bias,
        bias_up,
        bias_down,
    )
    sizes = [v.shape[0] for v in shards]
    lanes = w_qkv.shape[1] + w_out.shape[1]
    packed = jnp.concatenate(shards)
    used = packed.shape[0]
    packed = jnp.pad(packed, (0, -used % lanes)).reshape(-1, lanes)
    moved_qkv = lax.ppermute(w_qkv, ("dp", "ctx"), there)
    first = jnp.concatenate([jnp.concatenate([moved_qkv, w_out], axis=1), packed], axis=0)
    first = lax.all_gather(first, "dp", axis=0, tiled=False)
    part_rows, part_cols = w_qkv.shape
    vectors = first[:, part_rows:].reshape(dp, -1)[:, :used]
    full = []
    at = 0
    for size in sizes:
        full.append(vectors[:, at : at + size].reshape(dp * size).astype(jnp.float32))
        at += size
    (
        gain_one,
        shift_one,
        full_bias_qv,
        full_bias_out,
        gain_two,
        shift_two,
        full_bias_up,
        full_bias_down,
    ) = full

    qkv_c = columns_joined(first[:, :part_rows, :part_cols])
    out_c = (
        first[:, :part_rows, part_cols:].transpose(1, 0, 2).reshape(part_rows, dp * w_out.shape[1])
    )
    up_c = columns_whole(w_up)
    down_c = rows_whole(w_down)

    inputs = block_input.reshape(rows, width).astype(jnp.float32)
    scaled_one, inverse_one, _ = norm_forward(inputs, gain_one, shift_one)
    upstream = cotangent.reshape(rows, width)
    both = ctx_share(jnp.stack([block_input.reshape(rows, width), upstream]), 0)
    upstream_all = both[:, 1].reshape(tokens, width)
    inputs_all = both[:, 0].reshape(tokens, width).astype(jnp.float32)
    normed_one_all = norm_forward(inputs_all, gain_one, shift_one)[2]
    qkv_bias = jnp.concatenate(
        [full_bias_qv[:width], jnp.zeros((width,), jnp.float32), full_bias_qv[width:]]
    )
    span = qkv_c.shape[1]
    bias_c = lax.dynamic_slice_in_dim(qkv_bias, me * span, span)
    projected_c = (
        jnp.dot(normed_one_all, qkv_c, preferred_element_type=jnp.float32) + bias_c
    ).astype(low)
    projected = ctx_share(projected_c, 1)
    projected = (
        projected.reshape(ctx, ctx, seq_count, block_len, span)
        .transpose(2, 1, 3, 0, 4)
        .reshape(seq_count, seq_len, 3 * width)
    )
    queries = lax.dynamic_slice_in_dim(projected[:, :, :width], me * block_len, block_len, axis=1)
    query_heads = head_view(queries)
    key_heads = head_view(projected[:, :, width : 2 * width])
    value_heads = head_view(projected[:, :, 2 * width :])
    query_index = me * block_len + jnp.arange(block_len, dtype=jnp.int32)
    key_index = jnp.arange(seq_len, dtype=jnp.int32)
    allowed = key_index[None, :] <= query_index[:, None]
    scores = masked_scores(query_heads, key_heads, allowed, factor)
    peak = jnp.max(scores, axis=-1, keepdims=True)
    log_total = peak + jnp.log(jnp.sum(jnp.exp(scores - peak), axis=-1, keepdims=True))
    probs = jnp.exp(scores - log_total)
    soft_weights = probs.astype(low)
    mixed = jnp.einsum(
        "shqk,skhd->sqhd", soft_weights, value_heads, preferred_element_type=jnp.float32
    ).astype(low)

    slab = width // ctx

    def to_columns(block):
        wide = block.shape[1] // ctx
        swapped = block.reshape(rows, ctx, wide).transpose(1, 0, 2)
        return swapped

    mixed_c = ctx_swap(to_columns(mixed.reshape(rows, width)), 2).reshape(tokens, slab)
    out_part = jnp.dot(mixed_c, out_c, preferred_element_type=jnp.float32).astype(low).reshape(ctx, rows, width)
    out_sum = ctx_sum(out_part, 3)
    residual = inputs + (out_sum + full_bias_out)
    scaled_two, inverse_two, normed_two = norm_forward(residual, gain_two, shift_two)
    up_float = upstream.astype(jnp.float32)
    normed_two_all = ctx_share(normed_two, 4).reshape(tokens, width)
    units = up_c.shape[1]
    hidden_pre = jnp.dot(
        normed_two_all, up_c, preferred_element_type=jnp.float32
    ) + lax.dynamic_slice_in_dim(full_bias_up, me * units, units)
    hidden = gelu_value(hidden_pre).astype(low)
    down_part = outer_cols(hidden, down_c).astype(low).reshape(ctx, rows, width)
    grad_hidden = jnp.dot(
        upstream_all, down_c, preferred_element_type=jnp.float32
    ) * gelu_slope(hidden_pre)
    grad_hidden_low = grad_hidden.astype(low)
    normed_part = outer_cols(grad_hidden_low, up_c).astype(low).reshape(ctx, rows, width)
    sums = ctx_sum(jnp.stack([down_part, normed_part], axis=1), 5)
    down_grad = inner_rows(upstream_all, hidden).astype(low)
    up_grad = columns_split(inner_rows(normed_two_all, grad_hidden_low), w_up)
    down_grad, up_grad, sums = lax.optimization_barrier((down_grad, up_grad, sums))
    down_mine = lax.psum_scatter(down_grad, "dp", scatter_dimension=0, tiled=True)
    up_mine = lax.psum_scatter(up_grad, "dp", scatter_dimension=0, tiled=False)
    block_output = (
        (residual + (sums[0] + full_bias_down)).astype(low).reshape(seq_count, block_len, width)
    )
    grad_normed_two = sums[1]
    grad_residual = up_float + norm_backward(grad_normed_two, scaled_two, inverse_two, gain_two)
    grad_residual_low = grad_residual.astype(low)
    grad_residual_all = ctx_share(grad_residual_low, 6).reshape(tokens, width)
    grad_mixed_c = outer_cols(grad_residual_all, out_c).astype(low)
    grad_mixed = ctx_swap(grad_mixed_c.reshape(ctx, rows, slab), 7)
    grad_mixed = grad_mixed.transpose(1, 0, 2).reshape(seq_count, block_len, HEADS, HEAD_DIM)
    grad_probs = jnp.einsum(
        "sqhd,skhd->shqk", grad_mixed, value_heads, preferred_element_type=jnp.float32
    )
    delta = jnp.einsum("sqhd,sqhd->shq", grad_mixed, mixed, preferred_element_type=jnp.float32)[
        ..., None
    ]
    grad_scores = (probs * (grad_probs - delta) * factor).astype(low)
    grad_queries = jnp.einsum(
        "shqk,skhd->sqhd", grad_scores, key_heads, preferred_element_type=jnp.float32
    ).reshape(rows, width)
    key_part = jnp.einsum(
        "shqk,sqhd->skhd", grad_scores, query_heads, preferred_element_type=jnp.float32
    )
    value_part = jnp.einsum(
        "shqk,sqhd->skhd", soft_weights, grad_mixed, preferred_element_type=jnp.float32
    )

    def to_blocks(part):
        part = part.astype(low).reshape(seq_count, ctx, block_len, width)
        return part.transpose(1, 0, 2, 3).reshape(ctx, rows, width)

    pairs = jnp.stack([to_blocks(key_part), to_blocks(value_part)], axis=1)
    kv_sums = ctx_sum(pairs, 8)
    grad_keys, grad_values = kv_sums[0], kv_sums[1]
    grad_projected = jnp.concatenate([grad_queries, grad_keys, grad_values], axis=1).astype(low)
    grad_projected_c = ctx_swap(to_columns(grad_projected), 9).reshape(tokens, span)
    one_part = outer_cols(grad_projected_c, qkv_c).astype(low).reshape(ctx, rows, width)
    grad_normed_one = ctx_sum(one_part, 10)
    grad_input = grad_residual + norm_backward(grad_normed_one, scaled_one, inverse_one, gain_one)
    grad_input = grad_input.reshape(seq_count, block_len, width)

    grad_down = down_mine.T.astype(jnp.float32) * grad_scale
    grad_up = columns_back(up_mine)
    qkv_parts = columns_split(inner_rows(normed_one_all, grad_projected_c), w_qkv)
    out_parts = (
        inner_rows(grad_residual_all, mixed_c).astype(low).reshape(dp, w_out.shape[1], slab)
    )

    bias_up_c = jnp.sum(grad_hidden, axis=0)
    grad_bias_up = lax.dynamic_update_slice_in_dim(
        jnp.zeros((ctx * units,), jnp.float32), bias_up_c, me * units, axis=0
    )
    sums_here = (
        jnp.sum(grad_normed_one * scaled_one, axis=0),
        jnp.sum(grad_normed_one, axis=0),
        jnp.concatenate([jnp.sum(grad_queries, axis=0), jnp.sum(grad_values, axis=0)]),
        jnp.sum(grad_residual, axis=0),
        jnp.sum(grad_normed_two * scaled_two, axis=0),
        jnp.sum(grad_normed_two, axis=0),
        grad_bias_up,
        jnp.sum(up_float, axis=0),
    )
    table = jnp.concatenate([v.reshape(dp, -1) for v in sums_here], axis=1)
    table = jnp.sum(ctx_share(table, 11), axis=0)
    qkv_parts, out_parts, table = to_owners([qkv_parts, out_parts, table[:, None]], 12)
    grad_qkv = columns_back(jnp.sum(qkv_parts.astype(jnp.float32), axis=0))
    grad_out = jnp.sum(out_parts.astype(jnp.float32), axis=0).T * grad_scale
    totals = jnp.sum(table, axis=(0, 1)) * grad_scale
    owned = []
    at = 0
    for size in sizes:
        owned.append(totals[at : at + size])
        at += size
    return (
        block_output,
        grad_input,
        owned[0],
        owned[1],
        grad_qkv,
        owned[2],
        grad_out,
        owned[3],
        owned[4],
        owned[5],
        grad_up,
        owned[6],
        grad_down,
        owned[7],
    )


def solution(mesh):
    in_specs = (
        P("dp", "ctx", None),
        P("dp"),
        P("dp"),
        P("ctx", "dp"),
        P("dp"),
        P("ctx", "dp"),
        P("dp"),
        P("dp"),
        P("dp"),
        P("ctx", "dp"),
        P("dp"),
        P("ctx", "dp"),
        P("dp"),
        P("dp", "ctx", None),
    )
    out_specs = (
        P("dp", "ctx", None),
        P("dp", "ctx", None),
        P("dp"),
        P("dp"),
        P("ctx", "dp"),
        P("dp"),
        P("ctx", "dp"),
        P("dp"),
        P("dp"),
        P("dp"),
        P("ctx", "dp"),
        P("dp"),
        P("ctx", "dp"),
        P("dp"),
    )
    return jax.shard_map(
        on_device, mesh=mesh, in_specs=in_specs, out_specs=out_specs, check_vma=False
    )
```
